32 devices in a mesh: dp: 16 (over z, x, core), tensor: 2 (over y).
Axes of the slice: x: 2, y: 2, z: 4, core: 2. Of those that a mesh axis runs over, the one named last changes fastest.
Arguments:
- tokens: float32 [8224, 1024], P('dp')
- upstream: float32 [8224, 1024], P('dp'), may hold values from -6 to 6
- counts: int32 [16], P('dp'), may hold values from 0 to 2, as said below
- offsets: int32 [16, 2], P('dp'), may hold values from 0 to 257, as said below
- w_query: float32 [1024, 1024], P(None, 'tensor')
- w_key: float32 [1024, 1024], P(None, 'tensor')
- w_value: float32 [1024, 1024], P(None, 'tensor'), may hold values from -0.1875 to 0.1875
- w_out: float32 [1024, 1024], P('tensor'), may hold values from -0.375 to 0.375
- w_up: float32 [1024, 4096], P(None, 'tensor'), may hold values from -0.1875 to 0.1875
- w_down: float32 [4096, 1024], P('tensor'), may hold values from -0.09375 to 0.09375
- vectors: float32 [8, 1024], replicated, may hold values from -0.6 to 1.4
- attn_bias: float32 [2, 1024], P(None, 'tensor'), may hold values from -3 to 3
- up_bias: float32 [4096], P('tensor'), may hold values from -3 to 3
- mom_query: float32 [1024, 1024], P('dp', 'tensor'), may hold values from -48 to 48
- mom_key: float32 [1024, 1024], P('dp', 'tensor'), may hold values from -48 to 48
- mom_value: float32 [1024, 1024], P('dp', 'tensor'), may hold values from -48 to 48
- mom_out: float32 [1024, 1024], P(('tensor', 'dp')), may hold values from -48 to 48
- mom_up: float32 [1024, 4096], P('dp', 'tensor'), may hold values from -48 to 48
- mom_down: float32 [4096, 1024], P(('tensor', 'dp')), may hold values from -48 to 48
- mom_vectors: float32 [8, 1024], P(None, 'dp'), may hold values from -48 to 48
- mom_attn_bias: float32 [2, 1024], P(None, ('tensor', 'dp')), may hold values from -48 to 48
- mom_up_bias: float32 [4096], P(('tensor', 'dp')), may hold values from -48 to 48
Outputs:
- block_out: float32 [8224, 1024], P('dp')
- grad_tokens: float32 [8224, 1024], P('dp')
- grad_query: float32 [1024, 1024], P('dp', 'tensor')
- grad_key: float32 [1024, 1024], P('dp', 'tensor')
- grad_value: float32 [1024, 1024], P('dp', 'tensor')
- grad_out: float32 [1024, 1024], P(('tensor', 'dp'))
- grad_up: float32 [1024, 4096], P('dp', 'tensor')
- grad_down: float32 [4096, 1024], P(('tensor', 'dp'))
- grad_vectors: float32 [8, 1024], P(None, 'dp')
- grad_attn_bias: float32 [2, 1024], P(None, ('tensor', 'dp'))
- grad_up_bias: float32 [4096], P(('tensor', 'dp'))
- new_query: float32 [1024, 1024], P('dp', 'tensor')
- new_key: float32 [1024, 1024], P('dp', 'tensor')
- new_value: float32 [1024, 1024], P('dp', 'tensor')
- new_out: float32 [1024, 1024], P(('tensor', 'dp'))
- new_up: float32 [1024, 4096], P('dp', 'tensor')
- new_down: float32 [4096, 1024], P(('tensor', 'dp'))
- new_vectors: float32 [8, 1024], P(None, 'dp')
- new_attn_bias: float32 [2, 1024], P(None, ('tensor', 'dp'))
- new_up_bias: float32 [4096], P(('tensor', 'dp'))
- next_query: float32 [1024, 1024], P('dp', 'tensor')
- next_key: float32 [1024, 1024], P('dp', 'tensor')
- next_value: float32 [1024, 1024], P('dp', 'tensor')
- next_out: float32 [1024, 1024], P(('tensor', 'dp'))
- next_up: float32 [1024, 4096], P('dp', 'tensor')
- next_down: float32 [4096, 1024], P(('tensor', 'dp'))
- next_vectors: float32 [8, 1024], P(None, 'dp')
- next_attn_bias: float32 [2, 1024], P(None, ('tensor', 'dp'))
- next_up_bias: float32 [4096], P(('tensor', 'dp'))
The draws below stay inside these ranges and needn't reach their ends.
Inputs may be any that keep to these rules, and one draw needn't show every extreme that they name: `counts`: at least one data index holds 2 images and at least one holds none. For j < counts[d] the images of index d start at offsets[d, j], lie in order without intersecting within its 514 rows; entries at j >= counts[d] are 0.
All inputs are finite; a program needn't handle non-finite values.
Results may differ from the reference program's by a relative error of at most 0.039.
The reference program's roundings to bfloat16 on the way count: a program that leaves them out, or rounds other values in their place, can miss the bound.
Values may be sent and summed in bfloat16 or wider, within the bound.
No kernel may reach another device: no remote copies, remote signals or barrier semaphores. Data moves between devices by JAX's collectives and lax.ppermute only.
A program may use at most 320 MiB of HBM per device.

```python
import math
import jax
import jax.numpy as jnp
from jax import lax

D = 1024
HEADS = 16
FF = 4096
HEAD_DIM = 64
IMG_LEN = 257
SLOTS = 2
ROWS_DEV = 514
TOKENS = 8224
N_DP = 16
N_TENSOR = 2


def deal_images(key):
    base = jax.random.fold_in(key, 7)
    first_key, second_key, third_key = jax.random.split(base, 3)
    counts = jax.random.randint(first_key, (N_DP,), 0, SLOTS + 1)
    full_at = jax.random.randint(second_key, (), 0, N_DP)
    counts = counts.at[full_at].set(SLOTS)
    counts = counts.at[(full_at + 1) % N_DP].set(0)
    spare = (SLOTS - counts) * IMG_LEN
    start = jax.random.randint(third_key, (N_DP,), 0, 1048576) % (spare + 1)
    places = jnp.arange(SLOTS, dtype=jnp.int32)
    offsets = jnp.where(places[None, :] < counts[:, None], start[:, None] + places[None, :] * IMG_LEN, 0)
    return (counts.astype(jnp.int32), offsets.astype(jnp.int32))


def draw_counts(key, part):
    return deal_images(key)[0]


def draw_offsets(key, part):
    return deal_images(key)[1]


def draw_tokens(key, part):
    base = jax.random.normal(jax.random.fold_in(key, 3), (N_DP * ROWS_DEV, D), jnp.float32)
    return base


def query_key(key):
    key_part = jax.random.normal(jax.random.fold_in(key, 21), (D, D), jnp.float32) / math.sqrt(D)
    query_part = jax.random.normal(jax.random.fold_in(key, 22), (D, D), jnp.float32) / math.sqrt(D)
    return (query_part, key_part)


def draw_w_query(key, part):
    return query_key(key)[0]


def draw_w_key(key, part):
    return query_key(key)[1]


def draw_vectors(key, part):
    gains = jax.random.uniform(jax.random.fold_in(key, 31), (8, D), jnp.float32, 0.6, 1.4)
    shifts = jax.random.uniform(jax.random.fold_in(key, 32), (8, D), jnp.float32, -0.6, 0.6)
    layer_scales = jax.random.uniform(jax.random.fold_in(key, 33), (8, D), jnp.float32, 0.4, 1.2)
    kind = jnp.array([0, 1, 1, 2, 0, 1, 1, 2], jnp.int32)[:, None]
    return jnp.where(kind == 0, gains, jnp.where(kind == 1, shifts, layer_scales))


def level_of(own_key, shape, cuts, low, top_value):
    def one(position, blocks):
        steps = jax.random.uniform(jax.random.fold_in(jax.random.fold_in(own_key, 6), position), (blocks,), jnp.float32, low / len(cuts), top_value / len(cuts))
        return jnp.repeat(jnp.exp(steps), shape[position] // blocks).reshape((-1,) + (1,) * (len(shape) - position - 1))

    loudness = one(*cuts[0])
    for cut in cuts[1:]:
        loudness = loudness * one(*cut)
    return loudness


def bell_draw(stream_key, dims, scale, most, cuts=(), kind=jnp.bfloat16):
    values = scale * jax.random.normal(stream_key, dims, jnp.float32)
    if cuts:
        values = values * level_of(stream_key, dims, cuts, -0.22, 0.18)
    return jnp.clip(values, -most, most).astype(kind)


def setup_inputs(seed: int = 0) -> dict:
    arg_keys = jax.random.split(jax.random.key(seed), 23)
    return {
        "tokens": draw_tokens(jax.random.fold_in(arg_keys[22], 71), 0),
        "upstream": bell_draw(arg_keys[1], (TOKENS, D), 1.0, 6.0, ((0, 16),), jnp.float32),
        "counts": draw_counts(jax.random.fold_in(arg_keys[22], 71), 0),
        "offsets": draw_offsets(jax.random.fold_in(arg_keys[22], 71), 0),
        "w_query": draw_w_query(jax.random.fold_in(arg_keys[22], 71), 0),
        "w_key": draw_w_key(jax.random.fold_in(arg_keys[22], 71), 0),
        "w_value": bell_draw(arg_keys[6], (D, D), D ** -0.5, 0.1875, ((1, 2),), jnp.float32),
        "w_out": bell_draw(arg_keys[7], (D, D), (D // 4) ** -0.5, 0.375, ((0, 2),), jnp.float32),
        "w_up": bell_draw(arg_keys[8], (D, FF), D ** -0.5, 0.1875, ((1, 2),), jnp.float32),
        "w_down": bell_draw(arg_keys[9], (FF, D), FF ** -0.5, 0.09375, ((0, 2),), jnp.float32),
        "vectors": draw_vectors(jax.random.fold_in(arg_keys[22], 71), 0),
        "attn_bias": bell_draw(arg_keys[11], (2, D), 0.5, 3.0, ((1, 2),), jnp.float32),
        "up_bias": bell_draw(arg_keys[12], (FF,), 0.5, 3.0, ((0, 2),), jnp.float32),
        "mom_query": bell_draw(arg_keys[13], (D, D), 8.0, 48.0, ((0, 16), (1, 2)), jnp.float32),
        "mom_key": bell_draw(arg_keys[14], (D, D), 8.0, 48.0, ((0, 16), (1, 2)), jnp.float32),
        "mom_value": bell_draw(arg_keys[15], (D, D), 8.0, 48.0, ((0, 16), (1, 2)), jnp.float32),
        "mom_out": bell_draw(arg_keys[16], (D, D), 8.0, 48.0, ((0, 32),), jnp.float32),
        "mom_up": bell_draw(arg_keys[17], (D, FF), 8.0, 48.0, ((0, 16), (1, 2)), jnp.float32),
        "mom_down": bell_draw(arg_keys[18], (FF, D), 8.0, 48.0, ((0, 32),), jnp.float32),
        "mom_vectors": bell_draw(arg_keys[19], (8, D), 8.0, 48.0, ((1, 16),), jnp.float32),
        "mom_attn_bias": bell_draw(arg_keys[20], (2, D), 8.0, 48.0, ((1, 32),), jnp.float32),
        "mom_up_bias": bell_draw(arg_keys[21], (FF,), 8.0, 48.0, ((0, 32),), jnp.float32),
    }


norm_eps = 1e-06
momentum_beta = 0.9
matrix_rate = 0.2
vector_rate = 0.001
poly_first = 3.4445
poly_second = -4.775
poly_third = 2.0315

def widen(low):
    return lax.optimization_barrier(low).astype(jnp.float32)

def matmul(left, right):
    return jnp.dot(left, right, preferred_element_type=jnp.float32)

def layer_norm(rows):
    center = rows - lax.optimization_barrier(jnp.mean(rows, axis=-1, keepdims=True))
    inverse = lax.rsqrt(lax.optimization_barrier(jnp.mean(center * center, axis=-1, keepdims=True)) + norm_eps)
    return (center * inverse, inverse)

def norm_back(grad_normed, normed, inverse):
    return inverse * (grad_normed - lax.optimization_barrier(jnp.mean(grad_normed, axis=-1, keepdims=True)) - normed * lax.optimization_barrier(jnp.mean(grad_normed * normed, axis=-1, keepdims=True)))

def gelu_value(pre):
    return 0.5 * pre * (1.0 + lax.erf(pre * (1.0 / math.sqrt(2.0))))

def gelu_slope(pre):
    return 0.5 * (1.0 + lax.erf(pre * (1.0 / math.sqrt(2.0)))) + pre * jnp.exp(-0.5 * pre * pre) * (1.0 / math.sqrt(2.0 * math.pi))

def orthogonalize(block):
    flip = block.shape[0] > block.shape[1]
    current = block.T if flip else block
    wide = widen(current)
    current = (wide / (jnp.sqrt(jnp.sum(wide * wide)) + 1e-07)).astype(jnp.bfloat16)
    for step in range(5):
        gram = matmul(current, current.T).astype(jnp.bfloat16)
        poly = (poly_second * widen(gram) + poly_third * matmul(gram, gram)).astype(jnp.bfloat16)
        current = (poly_first * widen(current) + matmul(poly, current)).astype(jnp.bfloat16)
    return current.T if flip else current

def image_pass(rows, grad_out, weights):
    w_query, w_key, w_value, w_out, w_up, w_down, vectors, attn_bias, up_bias = weights
    count_rows = rows.shape[0]
    scale = 1.0 / math.sqrt(HEAD_DIM)
    normed1, inverse1 = layer_norm(rows)
    act1 = (normed1 * vectors[0] + vectors[1]).astype(jnp.bfloat16)
    query = (matmul(act1, w_query) + attn_bias[0]).astype(jnp.bfloat16)
    keys = matmul(act1, w_key).astype(jnp.bfloat16)
    values = (matmul(act1, w_value) + attn_bias[1]).astype(jnp.bfloat16)
    head_query = widen(query).reshape(count_rows, HEADS, HEAD_DIM)
    head_keys = widen(keys).reshape(count_rows, HEADS, HEAD_DIM)
    head_values = widen(values).reshape(count_rows, HEADS, HEAD_DIM)
    scores = jnp.einsum('qhd,khd->hqk', head_query, head_keys) * scale
    top = lax.optimization_barrier(jnp.max(scores, axis=-1, keepdims=True))
    log_total = top + jnp.log(lax.optimization_barrier(jnp.sum(jnp.exp(scores - top), axis=-1, keepdims=True)))
    probs = jnp.exp(scores - log_total)
    probs_low = probs.astype(jnp.bfloat16)
    mixed = jnp.einsum('hqk,khd->qhd', widen(probs_low), head_values).reshape(count_rows, D).astype(jnp.bfloat16)
    attn = matmul(mixed, w_out) + vectors[2]
    resid = rows + vectors[3] * attn
    normed2, inverse2 = layer_norm(resid)
    act2 = (normed2 * vectors[4] + vectors[5]).astype(jnp.bfloat16)
    pre = matmul(act2, w_up) + up_bias
    activ = gelu_value(pre).astype(jnp.bfloat16)
    mlp = matmul(activ, w_down) + vectors[6]
    out = resid + vectors[7] * mlp
    d_mlp = grad_out * vectors[7]
    d_mlp_low = d_mlp.astype(jnp.bfloat16)
    d_pre = matmul(d_mlp_low, w_down.T) * gelu_slope(pre)
    d_pre_low = d_pre.astype(jnp.bfloat16)
    d_act2 = matmul(d_pre_low, w_up.T)
    d_resid = grad_out + norm_back(d_act2 * vectors[4], normed2, inverse2)
    d_attn = d_resid * vectors[3]
    d_attn_low = d_attn.astype(jnp.bfloat16)
    d_mixed = matmul(d_attn_low, w_out.T).astype(jnp.bfloat16)
    head_dmix = widen(d_mixed).reshape(count_rows, HEADS, HEAD_DIM)
    d_values = jnp.einsum('hqk,qhd->khd', widen(probs_low), head_dmix).reshape(count_rows, D)
    d_probs = jnp.einsum('qhd,khd->hqk', head_dmix, head_values)
    delta = lax.optimization_barrier(jnp.sum(probs * d_probs, axis=-1, keepdims=True))
    d_scores = widen((probs * (d_probs - delta) * scale).astype(jnp.bfloat16))
    d_query = jnp.einsum('hqk,khd->qhd', d_scores, head_keys).reshape(count_rows, D)
    d_keys = jnp.einsum('hqk,qhd->khd', d_scores, head_query).reshape(count_rows, D)
    dq_low = d_query.astype(jnp.bfloat16)
    dk_low = d_keys.astype(jnp.bfloat16)
    dv_low = d_values.astype(jnp.bfloat16)
    d_act1 = matmul(dq_low, w_query.T) + matmul(dk_low, w_key.T) + matmul(dv_low, w_value.T)
    d_rows = d_resid + norm_back(d_act1 * vectors[0], normed1, inverse1)
    grads = (matmul(act1.T, dq_low), matmul(act1.T, dk_low), matmul(act1.T, dv_low), matmul(mixed.T, d_attn_low), matmul(act2.T, d_pre_low), matmul(activ.T, d_mlp_low), jnp.stack([lax.optimization_barrier(jnp.sum(d_act1 * normed1, axis=0)), lax.optimization_barrier(jnp.sum(d_act1, axis=0)), lax.optimization_barrier(jnp.sum(d_attn, axis=0)), lax.optimization_barrier(jnp.sum(d_resid * attn, axis=0)), lax.optimization_barrier(jnp.sum(d_act2 * normed2, axis=0)), lax.optimization_barrier(jnp.sum(d_act2, axis=0)), lax.optimization_barrier(jnp.sum(d_mlp, axis=0)), lax.optimization_barrier(jnp.sum(grad_out * mlp, axis=0))]), jnp.stack([lax.optimization_barrier(jnp.sum(d_query, axis=0)), lax.optimization_barrier(jnp.sum(d_values, axis=0))]), lax.optimization_barrier(jnp.sum(d_pre, axis=0)))
    return (out, d_rows, grads)

def reference(tokens, upstream, counts, offsets, w_query, w_key, w_value, w_out, w_up, w_down, vectors, attn_bias, up_bias, mom_query, mom_key, mom_value, mom_out, mom_up, mom_down, mom_vectors, mom_attn_bias, mom_up_bias):
    params = (w_query, w_key, w_value, w_out, w_up, w_down, vectors, attn_bias, up_bias)
    weights = tuple((p.astype(jnp.bfloat16) for p in params[:6])) + (vectors, attn_bias, up_bias)
    zero_grads = tuple((jnp.zeros(p.shape, jnp.float32) for p in params))

    def visit(carry, flat):
        device = flat // SLOTS
        place = flat % SLOTS
        live = place < counts[device]
        start = (device * ROWS_DEV + offsets[device, place]).astype(jnp.int32)

        def work(state):
            outputs, d_outputs, sums = state
            rows = lax.dynamic_slice_in_dim(tokens, start, IMG_LEN, 0)
            grad_rows = lax.dynamic_slice_in_dim(upstream, start, IMG_LEN, 0)
            result, d_rows, parts = image_pass(rows, grad_rows, weights)
            outputs = lax.dynamic_update_slice_in_dim(outputs, result, start, 0)
            d_outputs = lax.dynamic_update_slice_in_dim(d_outputs, d_rows, start, 0)
            sums = tuple((a + b for a, b in zip(sums, parts)))
            return (outputs, d_outputs, sums)

        def skip(state):
            return state
        return (lax.cond(live, work, skip, carry), None)
    start_state = (jnp.zeros(tokens.shape, jnp.float32), jnp.zeros(tokens.shape, jnp.float32), zero_grads)
    final_state, unused = lax.scan(visit, start_state, jnp.arange(N_DP * SLOTS, dtype=jnp.int32))
    block_out, grad_tokens, grads = final_state
    moments = (mom_query, mom_key, mom_value, mom_out, mom_up, mom_down, mom_vectors, mom_attn_bias, mom_up_bias)
    nexts = tuple((momentum_beta * m + g for m, g in zip(moments, grads)))
    split_axis = (1, 1, 1, 0, 1, 0)
    rates = (1.0, 1.0, 1.0, 1.0, math.sqrt(max(1.0, FF / D)), 1.0)
    updated = []
    for slot in range(6):
        low = nexts[slot].astype(jnp.bfloat16)
        shards = jnp.split(low, N_TENSOR, axis=split_axis[slot])
        ortho = jnp.concatenate([orthogonalize(s) for s in shards], axis=split_axis[slot])
        updated.append(params[slot] - matrix_rate * rates[slot] * widen(ortho))
    for slot in range(6, 9):
        updated.append(params[slot] - vector_rate * nexts[slot])
    return (block_out, grad_tokens, grads[0], grads[1], grads[2], grads[3], grads[4], grads[5], grads[6], grads[7], grads[8], updated[0], updated[1], updated[2], updated[3], updated[4], updated[5], updated[6], updated[7], updated[8], nexts[0], nexts[1], nexts[2], nexts[3], nexts[4], nexts[5], nexts[6], nexts[7], nexts[8])
```

```python
import math

import functools

import jax
import jax.numpy as jnp
from jax import lax
from jax.experimental import pallas as pl
from jax.experimental.pallas import tpu as pltpu
from jax.sharding import PartitionSpec as P

D = 1024
FF = 4096
HEAD_DIM = 64
IMG_LEN = 257
SLOTS = 2


norm_eps = 1e-06
momentum_beta = 0.9
matrix_rate = 0.2
vector_rate = 0.001
poly_first = 3.4445
poly_second = -4.775
poly_third = 2.0315


def matmul(left, right):
    return jnp.dot(left, right, preferred_element_type=jnp.float32)


def times_transposed(left, right):
    return lax.dot_general(
        left, right, (((1,), (1,)), ((), ())), preferred_element_type=jnp.float32
    )


def transposed_times(left, right):
    return lax.dot_general(
        left, right, (((0,), (0,)), ((), ())), preferred_element_type=jnp.float32
    )


def layer_norm(rows):
    center = rows - jnp.mean(rows, axis=-1, keepdims=True)
    inverse = lax.rsqrt(jnp.mean(center * center, axis=-1, keepdims=True) + norm_eps)
    return (center * inverse, inverse)


def norm_back(grad_normed, normed, inverse):
    return inverse * (
        grad_normed
        - jnp.mean(grad_normed, axis=-1, keepdims=True)
        - normed * jnp.mean(grad_normed * normed, axis=-1, keepdims=True)
    )


def gelu_value(pre):
    return 0.5 * pre * (1.0 + lax.erf(pre * (1.0 / math.sqrt(2.0))))


def gelu_slope(pre):
    return 0.5 * (1.0 + lax.erf(pre * (1.0 / math.sqrt(2.0)))) + pre * jnp.exp(-0.5 * pre * pre) * (
        1.0 / math.sqrt(2.0 * math.pi)
    )


def pair_sum(part):
    low = part.astype(jnp.bfloat16)
    if lax.axis_size("tensor") != 2:
        return lax.psum(low, "tensor").astype(jnp.float32)
    other = lax.ppermute(low, "tensor", [(0, 1), (1, 0)])
    return low.astype(jnp.float32) + other.astype(jnp.float32)


def newton_schulz(tall, x_ref, gram_ref, poly_ref, block=256, strip=512):
    side = gram_ref.shape[0]
    length = x_ref.shape[0] if tall else x_ref.shape[1]
    block, strip = min(block, side), min(strip, length)

    def gram_rows(low):
        if tall:
            return transposed_times(x_ref[:, low : low + block], x_ref[:, low:])
        return times_transposed(x_ref[low : low + block, :], x_ref[low:, :])

    def mirror(ref, low, rows):
        ref[low : low + block, low:] = rows
        for right in range(low + block, side, block):
            ref[right : right + block, low : low + block] = rows[
                :, right - low : right - low + block
            ].T

    def step(index, carry):
        for low in range(0, side, block):
            mirror(gram_ref, low, gram_rows(low).astype(jnp.bfloat16))
        for low in range(0, side, block):
            squares = matmul(gram_ref[low : low + block, :], gram_ref[:, low:])
            linear = gram_ref[low : low + block, low:].astype(jnp.float32)
            mirror(
                poly_ref, low, (poly_second * linear + poly_third * squares).astype(jnp.bfloat16)
            )
        for low in range(0, length, strip):
            part = (
                (slice(low, low + strip), slice(None))
                if tall
                else (slice(None), slice(low, low + strip))
            )
            old = x_ref[part]
            new = matmul(old, poly_ref[...]) if tall else matmul(poly_ref[...], old)
            x_ref[part] = (poly_first * old.astype(jnp.float32) + new).astype(jnp.bfloat16)
        return carry

    lax.fori_loop(0, 5, step, 0)


def ortho_kernel(tall, spots, in_ref, out_ref, x_ref, gram_ref, poly_ref):
    total = jnp.zeros((1, 1), jnp.float32)
    for (row, column, height, width), place, low in spots:
        piece = in_ref[place, low : low + height, :].astype(jnp.float32)
        total = total + jnp.sum(jnp.sum(piece * piece, axis=1, keepdims=True), axis=0, keepdims=True)
    norm = jnp.sqrt(total) + 1e-07
    for (row, column, height, width), place, low in spots:
        piece = in_ref[place, low : low + height, :].astype(jnp.float32)
        x_ref[row : row + height, column : column + width] = (piece / norm).astype(jnp.bfloat16)
    newton_schulz(tall, x_ref, gram_ref, poly_ref)
    for (row, column, height, width), place, low in spots:
        out_ref[place, low : low + height, :] = x_ref[
            row : row + height, column : column + width
        ]


def ortho_call(stack, shape, spots):
    tall = shape[0] > shape[1]
    side = min(shape)
    return pl.pallas_call(
        functools.partial(ortho_kernel, tall, spots),
        out_shape=jax.ShapeDtypeStruct(stack.shape, jnp.bfloat16),
        in_specs=[pl.BlockSpec(memory_space=pltpu.VMEM)],
        out_specs=pl.BlockSpec(memory_space=pltpu.VMEM),
        scratch_shapes=[
            pltpu.VMEM(shape, jnp.bfloat16),
            pltpu.VMEM((side, side), jnp.bfloat16),
            pltpu.VMEM((side, side), jnp.bfloat16),
        ],
        compiler_params=pltpu.CompilerParams(vmem_limit_bytes=48 * 1024 * 1024),
    )(stack)


class Grid:
    def __init__(self):
        self.size = lax.axis_size("dp")
        self.bits = self.size.bit_length() - 1
        self.me = lax.axis_index("dp")

    def bit(self, which):
        return (self.me >> which) & 1

    def swap(self, block, which):
        return lax.ppermute(
            block, "dp", [(d, d ^ (1 << which)) for d in range(self.size)]
        )

    def send(self, block, pairs):
        return lax.ppermute(block, "dp", pairs)


def pick(stack, index, axis):
    return lax.dynamic_index_in_dim(stack, index, axis, keepdims=False)


def scatter_sum(grid, part, order):
    rest = list(range(grid.bits - 1, -1, -1))
    held = part.reshape((2,) * grid.bits + part.shape[1:])
    for place, which in enumerate(order):
        axis = rest.index(which)
        rest.pop(axis)
        mine = grid.bit(which)
        sent = pick(held, 1 - mine, axis)
        came = grid.swap(sent, which)
        total = pick(held, mine, axis).astype(jnp.float32) + came.astype(jnp.float32)
        held = total if place == len(order) - 1 else total.astype(part.dtype)
    return held


def to_root(grid, held, roots):
    others = [held]
    low = grid.size >> grid.high
    for step in range(1, 1 << grid.high):
        pairs = [(((r ^ step) * low) + c, r * low + c) for c, r in enumerate(roots)]
        others.append(grid.send(held, pairs))
    return jnp.stack(others)


def from_root(grid, stack, roots):
    low = grid.size >> grid.high
    root = jnp.array(roots, jnp.int32)[grid.me % low]
    step_here = (grid.me // low) ^ root
    mine = stack[0]
    for step in range(1, 1 << grid.high):
        pairs = [(r * low + c, ((r ^ step) * low) + c) for c, r in enumerate(roots)]
        came = grid.send(stack[step], pairs)
        mine = jnp.where(step_here == step, came, mine)
    return mine


def fold(block):
    half = block.shape[1] // 2
    return jnp.concatenate([block[:, :half], block[:, half:]], axis=0)


def unfold(block):
    half = block.shape[0] // 2
    return jnp.concatenate([block[:half], block[half:]], axis=1)


def pair_pass(rows, grad_out, weights):
    w_query, w_key, w_value, w_out, w_up, w_down, vectors, attn_bias, up_bias = weights
    total_rows = rows.shape[0]
    pieces = total_rows // IMG_LEN
    local_width = w_query.shape[1]
    heads_here = local_width // HEAD_DIM
    scale = 1.0 / math.sqrt(HEAD_DIM)

    def split_heads(block):
        return block.reshape(pieces, IMG_LEN, heads_here, HEAD_DIM)

    def join_heads(block):
        return block.reshape(total_rows, local_width)

    normed1, inverse1 = layer_norm(rows)
    act1 = (normed1 * vectors[0] + vectors[1]).astype(jnp.bfloat16)
    query = (matmul(act1, w_query) + attn_bias[0]).astype(jnp.bfloat16)
    keys = matmul(act1, w_key).astype(jnp.bfloat16)
    values = (matmul(act1, w_value) + attn_bias[1]).astype(jnp.bfloat16)
    head_query = split_heads(query)
    head_keys = split_heads(keys)
    head_values = split_heads(values)
    scores = (
        jnp.einsum("bqhd,bkhd->bhqk", head_query, head_keys, preferred_element_type=jnp.float32)
        * scale
    )
    top = jnp.max(scores, axis=-1, keepdims=True)
    log_total = top + jnp.log(jnp.sum(jnp.exp(scores - top), axis=-1, keepdims=True))
    probs_low = jnp.exp(scores - log_total).astype(jnp.bfloat16)
    mixed = join_heads(
        jnp.einsum("bhqk,bkhd->bqhd", probs_low, head_values, preferred_element_type=jnp.float32)
    ).astype(jnp.bfloat16)
    attn = (
        pair_sum(matmul(mixed, w_out))
        + vectors[2]
    )
    resid = rows + vectors[3] * attn
    normed2, inverse2 = layer_norm(resid)
    act2 = (normed2 * vectors[4] + vectors[5]).astype(jnp.bfloat16)
    pre = matmul(act2, w_up) + up_bias
    activ = gelu_value(pre).astype(jnp.bfloat16)
    mlp = (
        pair_sum(matmul(activ, w_down))
        + vectors[6]
    )
    result = resid + vectors[7] * mlp
    d_mlp = grad_out * vectors[7]
    d_mlp_low = d_mlp.astype(jnp.bfloat16)
    d_pre = times_transposed(d_mlp_low, w_down) * gelu_slope(pre)
    d_pre_low = d_pre.astype(jnp.bfloat16)
    d_act2 = pair_sum(times_transposed(d_pre_low, w_up))
    d_resid = grad_out + norm_back(d_act2 * vectors[4], normed2, inverse2)
    d_attn = d_resid * vectors[3]
    d_attn_low = d_attn.astype(jnp.bfloat16)
    d_mixed = split_heads(times_transposed(d_attn_low, w_out).astype(jnp.bfloat16))
    again = (
        jnp.einsum("bqhd,bkhd->bhqk", head_query, head_keys, preferred_element_type=jnp.float32)
        * scale
    )
    probs = jnp.exp(again - log_total)
    probs_again = probs.astype(jnp.bfloat16)
    d_values = join_heads(
        jnp.einsum("bhqk,bqhd->bkhd", probs_again, d_mixed, preferred_element_type=jnp.float32)
    )
    d_probs = jnp.einsum(
        "bqhd,bkhd->bhqk", d_mixed, head_values, preferred_element_type=jnp.float32
    )
    delta = jnp.sum(probs * d_probs, axis=-1, keepdims=True)
    d_scores = (probs * (d_probs - delta) * scale).astype(jnp.bfloat16)
    d_query = join_heads(
        jnp.einsum("bhqk,bkhd->bqhd", d_scores, head_keys, preferred_element_type=jnp.float32)
    )
    d_keys = join_heads(
        jnp.einsum("bhqk,bqhd->bkhd", d_scores, head_query, preferred_element_type=jnp.float32)
    )
    dq_low = d_query.astype(jnp.bfloat16)
    dk_low = d_keys.astype(jnp.bfloat16)
    dv_low = d_values.astype(jnp.bfloat16)
    local_back = (
        times_transposed(dq_low, w_query)
        + times_transposed(dk_low, w_key)
        + times_transposed(dv_low, w_value)
    )
    d_act1 = pair_sum(local_back)
    d_rows = d_resid + norm_back(d_act1 * vectors[0], normed1, inverse1)
    grads = (
        transposed_times(act1, dq_low),
        transposed_times(act1, dk_low),
        transposed_times(act1, dv_low),
        transposed_times(mixed, d_attn_low),
        transposed_times(act2, d_pre_low),
        transposed_times(activ, d_mlp_low),
        jnp.stack(
            [
                jnp.sum(d_act1 * normed1, axis=0),
                jnp.sum(d_act1, axis=0),
                jnp.sum(d_attn, axis=0),
                jnp.sum(d_resid * attn, axis=0),
                jnp.sum(d_act2 * normed2, axis=0),
                jnp.sum(d_act2, axis=0),
                jnp.sum(d_mlp, axis=0),
                jnp.sum(grad_out * mlp, axis=0),
            ]
        ),
        jnp.stack([jnp.sum(d_query, axis=0), jnp.sum(d_values, axis=0)]),
        jnp.sum(d_pre, axis=0),
    )
    return (result, d_rows, grads)


def place_rows(buffer, block, start, live):
    current = lax.dynamic_slice_in_dim(buffer, start, IMG_LEN, 0)
    return lax.dynamic_update_slice_in_dim(buffer, jnp.where(live, block, current), start, 0)


def local(
    tokens,
    upstream,
    counts,
    offsets,
    w_query,
    w_key,
    w_value,
    w_out,
    w_up,
    w_down,
    vectors,
    attn_bias,
    up_bias,
    mom_query,
    mom_key,
    mom_value,
    mom_out,
    mom_up,
    mom_down,
    mom_vectors,
    mom_attn_bias,
    mom_up_bias,
):
    params = (w_query, w_key, w_value, w_out, w_up, w_down, vectors, attn_bias, up_bias)
    weights = tuple((p.astype(jnp.bfloat16) for p in params[:6])) + (vectors, attn_bias, up_bias)
    image_count = counts[0]
    first, second = offsets[0, 0], offsets[0, 1]
    first_live = 0 < image_count
    second_live = 1 < image_count
    rows = jnp.concatenate(
        [
            lax.dynamic_slice_in_dim(tokens, first, IMG_LEN, 0),
            lax.dynamic_slice_in_dim(tokens, second, IMG_LEN, 0),
        ],
        axis=0,
    )
    grad_rows = jnp.concatenate(
        [
            lax.dynamic_slice_in_dim(upstream, first, IMG_LEN, 0) * first_live.astype(jnp.float32),
            lax.dynamic_slice_in_dim(upstream, second, IMG_LEN, 0)
            * second_live.astype(jnp.float32),
        ],
        axis=0,
    )
    result, d_rows, grads = pair_pass(rows, grad_rows, weights)
    block_out = jnp.zeros(tokens.shape, jnp.float32)
    grad_tokens = jnp.zeros(tokens.shape, jnp.float32)
    block_out = place_rows(block_out, result[IMG_LEN:], second, second_live)
    block_out = place_rows(block_out, result[:IMG_LEN], first, first_live)
    grad_tokens = place_rows(grad_tokens, d_rows[IMG_LEN:], second, second_live)
    grad_tokens = place_rows(grad_tokens, d_rows[:IMG_LEN], first, first_live)

    grid = Grid()
    size, bits, me = grid.size, grid.bits, grid.me
    order_a = list(range(bits))
    order_b = [0] + list(range(2, bits)) + [1]
    bf16 = jnp.bfloat16

    def blocks(full):
        return full.reshape((size, full.shape[0] // size) + full.shape[1:])

    def own_rows(full):
        width = full.shape[0] // size
        return lax.dynamic_slice_in_dim(full, me * width, width, 0)

    def own_columns(full):
        return own_rows(full.T).T

    g_up = scatter_sum(grid, blocks(grads[4].astype(bf16)), order_a)
    g_down = scatter_sum(grid, blocks(grads[5].astype(bf16)), order_b)
    g_query = scatter_sum(grid, blocks(grads[0].astype(bf16)), order_a)
    g_key = scatter_sum(grid, blocks(grads[1].astype(bf16)), order_b)
    g_value = scatter_sum(grid, blocks(grads[2].astype(bf16)), order_a)
    g_out = scatter_sum(grid, blocks(grads[3].astype(bf16)), order_b)

    def by_columns(full):
        height, width = full.shape
        return full.reshape(height, size, width // size).transpose(1, 0, 2).reshape(size, -1)

    vec_part = by_columns(grads[6])
    bias_part = by_columns(grads[7])
    upb_part = grads[8].reshape(size, -1)
    packed = jnp.concatenate([vec_part, bias_part, upb_part], axis=1)
    fill = -packed.shape[1] % 128
    packed = jnp.pad(packed, ((0, 0), (0, fill))).reshape(size, -1, 128)
    small = scatter_sum(grid, packed, order_a).reshape(-1)
    n_vec, n_bias, n_upb = vec_part.shape[1], bias_part.shape[1], upb_part.shape[1]
    grad_vec = small[:n_vec].reshape(vectors.shape[0], -1)
    grad_bias = small[n_vec : n_vec + n_bias].reshape(attn_bias.shape[0], -1)
    grad_upb = small[n_vec + n_bias : n_vec + n_bias + n_upb]

    grad_shares = (g_query, g_key, g_value, g_out, g_up, g_down)
    old_moments = (mom_query, mom_key, mom_value, mom_out, mom_up, mom_down)
    next_mats = tuple((momentum_beta * m + g for m, g in zip(old_moments, grad_shares)))
    next_vec = momentum_beta * mom_vectors + grad_vec
    next_bias = momentum_beta * mom_attn_bias + grad_bias
    next_upb = momentum_beta * mom_up_bias + grad_upb
    low = tuple((m.astype(bf16) for m in next_mats))

    grid.high = bits - 2
    highs = 1 << grid.high
    column, core = grid.bit(1), grid.bit(0)
    high_a, high_b = min(1, highs - 1), min(2, highs - 1)

    big_roots = (high_a, high_a, high_b, high_b)
    up_share, down_share = fold(low[4]), low[5]
    keep = jnp.where(column == 0, up_share, down_share)
    came = grid.swap(jnp.where(column == 0, down_share, up_share), 1)
    held = to_root(grid, jnp.stack([keep, came]), big_roots)
    big_stack = jnp.stack([held, grid.send(held, [((r << 2) | (c << 1) | 1, (r << 2) | (c << 1)) for c, r in ((0, high_a), (1, high_b))])])
    up_root, down_root = high_a << 2, (high_b << 2) | 2

    small_roots = (high_b, high_a, high_a, high_b)
    shares = [low[0], low[1], low[2], fold(low[3])]
    first_pair, second_pair = jnp.stack(shares[:2]), jnp.stack(shares[2:])
    keep = jnp.where(column == 0, first_pair, second_pair)
    came = grid.swap(jnp.where(column == 0, second_pair, first_pair), 1)
    two = jnp.stack([keep, came], axis=1)
    keep = pick(two, core, 0)
    came = grid.swap(pick(two, 1 - core, 0), 0)
    small_stack = to_root(grid, jnp.stack([keep, came]), small_roots)
    small_devices = [(r << 2) | c for c, r in enumerate(small_roots)]

    def big_spots(root, shape, folded):
        height, width = shape[0] // size, shape[1]
        spots = []
        for d in range(size):
            place = (
                ((d & 1) ^ (root & 1)) * highs + ((d >> 2) ^ (root >> 2))
            ) * 2 + (((d >> 1) ^ (root >> 1)) & 1)
            if folded:
                spots.append(((d * height, 0, height, width // 2), place, 0))
                spots.append(((d * height, width // 2, height, width // 2), place, height))
            else:
                spots.append(((d * height, 0, height, width), place, 0))
        return spots

    def small_spots(root, shape, folded):
        height, width = shape[0] // size, shape[1]
        spots = []
        for d in range(size):
            place = (
                ((d >> 2) ^ (root >> 2)) * 2 + ((d & 1) ^ (root & 1))
            ) * 2 + (((d >> 1) ^ (root >> 1)) & 1)
            if folded:
                spots.append(((d * height, 0, height, width // 2), place, 0))
                spots.append(((d * height, width // 2, height, width // 2), place, height))
            else:
                spots.append(((d * height, 0, height, width), place, 0))
        return spots

    def flat(stack):
        return stack.reshape((-1,) + stack.shape[-2:])

    role = jnp.where(me == up_root, 1, jnp.where(me == down_root, 2, 0))
    big_flat = lax.switch(
        role,
        [
            lambda s: s,
            lambda s: ortho_call(s, w_up.shape, big_spots(up_root, w_up.shape, True)),
            lambda s: ortho_call(s, w_down.shape, big_spots(down_root, w_down.shape, False)),
        ],
        flat(big_stack),
    )
    role = jnp.where(
        me == small_devices[3],
        4,
        jnp.where(
            me == small_devices[0],
            1,
            jnp.where(me == small_devices[1], 2, jnp.where(me == small_devices[2], 3, 0)),
        ),
    )
    small_flat = lax.switch(
        role,
        [lambda s: s]
        + [
            functools.partial(
                lambda root, s: ortho_call(s, w_query.shape, small_spots(root, w_query.shape, False)),
                root,
            )
            for root in small_devices[:3]
        ]
        + [
            lambda s: ortho_call(
                s, w_out.shape, small_spots(small_devices[3], w_out.shape, True)
            )
        ],
        flat(small_stack),
    )

    big = big_flat.reshape(big_stack.shape)
    came = grid.send(big[1], [((r << 2) | (c << 1), (r << 2) | (c << 1) | 1) for c, r in ((0, high_a), (1, high_b))])
    held = jnp.where(core == 0, big[0], came)
    held = from_root(grid, held, big_roots)
    came = grid.swap(held[1], 1)
    up_ortho = unfold(jnp.where(column == 0, held[0], came))
    down_ortho = jnp.where(column == 0, came, held[0])

    held = from_root(grid, small_flat.reshape(small_stack.shape), small_roots)
    came = grid.swap(held[1], 0)
    two = jnp.where(core == 0, jnp.stack([held[0], came]), jnp.stack([came, held[0]]))
    came = grid.swap(two[:, 1], 1)
    first_pair = jnp.where(column == 0, two[:, 0], came)
    second_pair = jnp.where(column == 0, came, two[:, 0])
    orthos = (
        first_pair[0],
        first_pair[1],
        second_pair[0],
        unfold(second_pair[1]),
        up_ortho,
        down_ortho,
    )
    rates = (1.0, 1.0, 1.0, 1.0, math.sqrt(max(1.0, FF / D)), 1.0)
    updated = []
    for slot in range(6):
        updated.append(
            own_rows(params[slot]) - matrix_rate * rates[slot] * orthos[slot].astype(jnp.float32)
        )
    new_vectors = own_columns(vectors) - vector_rate * next_vec
    new_bias = own_columns(attn_bias) - vector_rate * next_bias
    new_upb = own_rows(up_bias) - vector_rate * next_upb
    return (
        block_out,
        grad_tokens,
        *grad_shares,
        grad_vec,
        grad_bias,
        grad_upb,
        *updated,
        new_vectors,
        new_bias,
        new_upb,
        *next_mats,
        next_vec,
        next_bias,
        next_upb,
    )


def solution(mesh):
    placed = (
        P("dp", None),
        P("dp", None),
        P("dp"),
        P("dp", None),
        P(None, "tensor"),
        P(None, "tensor"),
        P(None, "tensor"),
        P("tensor", None),
        P(None, "tensor"),
        P("tensor", None),
        P(),
        P(None, "tensor"),
        P("tensor"),
        P("dp", "tensor"),
        P("dp", "tensor"),
        P("dp", "tensor"),
        P(("tensor", "dp"), None),
        P("dp", "tensor"),
        P(("tensor", "dp"), None),
        P(None, "dp"),
        P(None, ("tensor", "dp")),
        P(("tensor", "dp")),
    )
    return jax.shard_map(
        local,
        mesh=mesh,
        in_specs=placed,
        out_specs=(
            P("dp", None),
            P("dp", None),
            P("dp", "tensor"),
            P("dp", "tensor"),
            P("dp", "tensor"),
            P(("tensor", "dp"), None),
            P("dp", "tensor"),
            P(("tensor", "dp"), None),
            P(None, "dp"),
            P(None, ("tensor", "dp")),
            P(("tensor", "dp")),
            P("dp", "tensor"),
            P("dp", "tensor"),
            P("dp", "tensor"),
            P(("tensor", "dp"), None),
            P("dp", "tensor"),
            P(("tensor", "dp"), None),
            P(None, "dp"),
            P(None, ("tensor", "dp")),
            P(("tensor", "dp")),
            P("dp", "tensor"),
            P("dp", "tensor"),
            P("dp", "tensor"),
            P(("tensor", "dp"), None),
            P("dp", "tensor"),
            P(("tensor", "dp"), None),
            P(None, "dp"),
            P(None, ("tensor", "dp")),
            P(("tensor", "dp")),
        ),
        check_vma=False,
    )
```

```python
import math

import functools

import jax
import jax.numpy as jnp
from jax import lax
from jax.experimental import pallas as pl
from jax.experimental.pallas import tpu as pltpu
from jax.sharding import PartitionSpec as P

D = 1024
FF = 4096
HEAD_DIM = 64
IMG_LEN = 257
SLOTS = 2


norm_eps = 1e-06
momentum_beta = 0.9
matrix_rate = 0.2
vector_rate = 0.001
poly_first = 3.4445
poly_second = -4.775
poly_third = 2.0315


def matmul(left, right):
    return jnp.dot(left, right, preferred_element_type=jnp.float32)


def times_transposed(left, right):
    return lax.dot_general(
        left, right, (((1,), (1,)), ((), ())), preferred_element_type=jnp.float32
    )


def transposed_times(left, right):
    return lax.dot_general(
        left, right, (((0,), (0,)), ((), ())), preferred_element_type=jnp.float32
    )


def layer_norm(rows):
    center = rows - jnp.mean(rows, axis=-1, keepdims=True)
    inverse = lax.rsqrt(jnp.mean(center * center, axis=-1, keepdims=True) + norm_eps)
    return (center * inverse, inverse)


def norm_back(grad_normed, normed, inverse):
    return inverse * (
        grad_normed
        - jnp.mean(grad_normed, axis=-1, keepdims=True)
        - normed * jnp.mean(grad_normed * normed, axis=-1, keepdims=True)
    )


SUBLANES = 8
TILE = 16
LANES = 128
VMEM_LIMIT = 56 * 1024 * 1024
F32 = jnp.float32
BF16 = jnp.bfloat16
MASKED = -1e30


def vmem():
    return pl.BlockSpec(memory_space=pltpu.VMEM)


def smem():
    return pl.BlockSpec(memory_space=pltpu.SMEM)


def padded_rows():
    return -(-IMG_LEN // TILE) * TILE


def window_rows(total):
    return (total - IMG_LEN) // SUBLANES * SUBLANES + padded_rows() + SUBLANES


def take_image(src_ref, pad_ref, start, live):
    total = src_ref.shape[0]
    size = padded_rows() + SUBLANES
    pad_ref[0:total, :] = src_ref[...]
    pad_ref[total:, :] = jnp.zeros((pad_ref.shape[0] - total, pad_ref.shape[1]), F32)
    base = (start >> 3) << 3
    window = pad_ref[pl.ds(pl.multiple_of(base, SUBLANES), size), :]
    rows = pltpu.roll(window, lax.rem(size - (start - base), size), axis=0)[: padded_rows()]
    index = lax.broadcasted_iota(jnp.int32, (padded_rows(), 1), 0)
    return jnp.where((index < IMG_LEN) & live, rows, 0.0)


def row_sum(block):
    return jnp.sum(block, axis=0, keepdims=True)


def half_masks():
    lane = lax.broadcasted_iota(jnp.int32, (1, LANES), 1)
    return [(lane < HEAD_DIM).astype(F32).astype(BF16), (lane >= HEAD_DIM).astype(F32).astype(BF16)]


def head_scores(keys_half, query_pair):
    scores = times_transposed(keys_half, query_pair) * (1.0 / math.sqrt(HEAD_DIM))
    index = lax.broadcasted_iota(jnp.int32, (scores.shape[0], 1), 0)
    return jnp.where(index < IMG_LEN, scores, MASKED)


def attend_kernel(
    place_ref,
    tokens_ref,
    w_query_ref,
    w_key_ref,
    w_value_ref,
    w_out_ref,
    vectors_ref,
    bias_ref,
    rows_ref,
    act_ref,
    query_ref,
    keys_ref,
    values_ref,
    mixed_ref,
    lse_ref,
    part_ref,
    pad_ref,
    turned_ref,
    mixed_turned_ref,
):
    rows = take_image(tokens_ref, pad_ref, place_ref[0], True)
    rows_ref[...] = rows
    normed, inverse = layer_norm(rows)
    index = lax.broadcasted_iota(jnp.int32, (rows.shape[0], 1), 0)
    act = jnp.where(index < IMG_LEN, normed * vectors_ref[0:1, :] + vectors_ref[1:2, :], 0.0)
    act = act.astype(BF16)
    act_ref[...] = act
    query_ref[...] = (matmul(act, w_query_ref[...].astype(BF16)) + bias_ref[0:1, :]).astype(BF16)
    keys_ref[...] = matmul(act, w_key_ref[...].astype(BF16)).astype(BF16)
    values = matmul(act, w_value_ref[...].astype(BF16)) + bias_ref[1:2, :]
    values_ref[...] = values.astype(BF16)
    turned_ref[...] = values.T.astype(BF16)
    masks = half_masks()

    def pair(index, carry):
        low = pl.multiple_of(index * LANES, LANES)
        query_pair = query_ref[:, pl.ds(low, LANES)]
        keys_pair = keys_ref[:, pl.ds(low, LANES)]
        for half in range(2):
            scores = head_scores(keys_pair * masks[half], query_pair)
            top = jnp.max(scores, axis=0, keepdims=True)
            raised = jnp.exp(scores - top)
            total = row_sum(raised)
            probs = (raised * (1.0 / total)).astype(BF16)
            at = pl.multiple_of(low + half * HEAD_DIM, HEAD_DIM)
            mixed_turned_ref[pl.ds(at, HEAD_DIM), :] = matmul(
                turned_ref[pl.ds(at, HEAD_DIM), :], probs
            )
            lse_ref[pl.ds(2 * index + half, 1), :] = top + jnp.log(total)
        return carry

    lax.fori_loop(0, query_ref.shape[1] // LANES, pair, 0)
    mixed = mixed_turned_ref[...].T.astype(BF16)
    mixed_ref[...] = mixed
    part_ref[...] = matmul(mixed, w_out_ref[...].astype(BF16)).astype(BF16)


def attend(start, tokens, w_query, w_key, w_value, w_out, vectors, attn_bias):
    rows, width, inner = padded_rows(), tokens.shape[1], w_query.shape[1]
    return pl.pallas_call(
        attend_kernel,
        out_shape=(
            jax.ShapeDtypeStruct((rows, width), F32),
            jax.ShapeDtypeStruct((rows, width), BF16),
            jax.ShapeDtypeStruct((rows, inner), BF16),
            jax.ShapeDtypeStruct((rows, inner), BF16),
            jax.ShapeDtypeStruct((rows, inner), BF16),
            jax.ShapeDtypeStruct((rows, inner), BF16),
            jax.ShapeDtypeStruct((inner // HEAD_DIM, rows), F32),
            jax.ShapeDtypeStruct((rows, width), BF16),
        ),
        in_specs=[smem()] + [vmem()] * 7,
        out_specs=(vmem(),) * 8,
        scratch_shapes=[
            pltpu.VMEM((window_rows(tokens.shape[0]), width), F32),
            pltpu.VMEM((inner, rows), BF16),
            pltpu.VMEM((inner, rows), F32),
        ],
        compiler_params=pltpu.CompilerParams(vmem_limit_bytes=VMEM_LIMIT),
        cost_estimate=pl.CostEstimate(
            flops=10 * rows * width * inner, bytes_accessed=20 * width * inner, transcendentals=0
        ),
        name="attend",
    )(start, tokens, w_query, w_key, w_value, w_out, vectors, attn_bias)


def feed_kernel(
    place_ref,
    own_ref,
    other_ref,
    rows_ref,
    upstream_ref,
    vectors_ref,
    up_bias_ref,
    w_up_ref,
    w_down_ref,
    resid_ref,
    grad_ref,
    act_ref,
    d_mlp_ref,
    activ_ref,
    d_pre_ref,
    bias_sum_ref,
    d_act_part_ref,
    mlp_part_ref,
    pad_ref,
    d_act_sum_ref,
    mlp_sum_ref,
):
    step = pl.program_id(0)

    @pl.when(step == 0)
    def _():
        attn = own_ref[...].astype(F32) + other_ref[...].astype(F32) + vectors_ref[2:3, :]
        resid = rows_ref[...] + vectors_ref[3:4, :] * attn
        resid_ref[...] = resid
        normed, inverse = layer_norm(resid)
        act_ref[...] = (normed * vectors_ref[4:5, :] + vectors_ref[5:6, :]).astype(BF16)
        grad = take_image(upstream_ref, pad_ref, place_ref[0], place_ref[1] > 0)
        grad_ref[...] = grad
        d_mlp_ref[...] = (grad * vectors_ref[7:8, :]).astype(BF16)
        d_act_sum_ref[...] = jnp.zeros(d_act_sum_ref.shape, F32)
        mlp_sum_ref[...] = jnp.zeros(mlp_sum_ref.shape, F32)

    w_up = w_up_ref[...].astype(BF16)
    w_down = w_down_ref[...].astype(BF16)
    pre = matmul(act_ref[...], w_up) + up_bias_ref[...]
    error = lax.erf(pre * (1.0 / math.sqrt(2.0)))
    bell = jnp.exp(-0.5 * pre * pre) * (1.0 / math.sqrt(2.0 * math.pi))
    half = 0.5 * (1.0 + error)
    activ = (pre * half).astype(BF16)
    activ_ref[...] = activ
    d_pre = times_transposed(d_mlp_ref[...], w_down) * (half + pre * bell)
    bias_sum_ref[...] = row_sum(d_pre)
    d_pre = d_pre.astype(BF16)
    d_pre_ref[...] = d_pre
    d_act_sum_ref[...] += times_transposed(d_pre, w_up)
    mlp_sum_ref[...] += matmul(activ, w_down)

    @pl.when(step == pl.num_programs(0) - 1)
    def _():
        d_act_part_ref[...] = d_act_sum_ref[...].astype(BF16)
        mlp_part_ref[...] = mlp_sum_ref[...].astype(BF16)


def feed(place, own, other, image_rows, upstream, vectors, up_bias, w_up, w_down, steps=4):
    rows, width = image_rows.shape
    hidden = w_up.shape[1]
    chunk = hidden // steps
    whole = lambda *shape: pl.BlockSpec(shape, lambda c: (0,) * len(shape))
    return pl.pallas_call(
        feed_kernel,
        grid=(steps,),
        out_shape=(
            jax.ShapeDtypeStruct((rows, width), F32),
            jax.ShapeDtypeStruct((rows, width), F32),
            jax.ShapeDtypeStruct((rows, width), BF16),
            jax.ShapeDtypeStruct((rows, width), BF16),
            jax.ShapeDtypeStruct((rows, hidden), BF16),
            jax.ShapeDtypeStruct((rows, hidden), BF16),
            jax.ShapeDtypeStruct((1, hidden), F32),
            jax.ShapeDtypeStruct((rows, width), BF16),
            jax.ShapeDtypeStruct((rows, width), BF16),
        ),
        in_specs=[
            smem(),
            whole(rows, width),
            whole(rows, width),
            whole(rows, width),
            whole(*upstream.shape),
            whole(*vectors.shape),
            pl.BlockSpec((1, chunk), lambda c: (0, c)),
            pl.BlockSpec((width, chunk), lambda c: (0, c)),
            pl.BlockSpec((chunk, width), lambda c: (c, 0)),
        ],
        out_specs=(
            whole(rows, width),
            whole(rows, width),
            whole(rows, width),
            whole(rows, width),
            pl.BlockSpec((rows, chunk), lambda c: (0, c)),
            pl.BlockSpec((rows, chunk), lambda c: (0, c)),
            pl.BlockSpec((1, chunk), lambda c: (0, c)),
            whole(rows, width),
            whole(rows, width),
        ),
        scratch_shapes=[
            pltpu.VMEM((window_rows(upstream.shape[0]), width), F32),
            pltpu.VMEM((rows, width), F32),
            pltpu.VMEM((rows, width), F32),
        ],
        compiler_params=pltpu.CompilerParams(vmem_limit_bytes=VMEM_LIMIT),
        cost_estimate=pl.CostEstimate(
            flops=8 * rows * width * hidden,
            bytes_accessed=8 * width * hidden,
            transcendentals=2 * rows * hidden,
        ),
        name="feed",
    )(place, own, other, image_rows, upstream, vectors, up_bias, w_up, w_down)


def split_parity(block, height, core, send_ref, keep_ref, first):
    for index in range(block.shape[0] // (2 * height)):
        low = 2 * height * index
        even, odd = block[low : low + height], block[low + height : low + 2 * height]
        send_ref[first + index] = jnp.where(core == 0, odd, even)
        keep_ref[first + index] = jnp.where(core == 0, even, odd)


def both(first_ref, second_ref):
    return jnp.concatenate([first_ref[...], second_ref[...]], axis=0)


def big_grad_kernel(height, core_ref, left0_ref, left1_ref, right0_ref, right1_ref, send_ref, keep_ref, right_ref):
    core = core_ref[0]

    @pl.when(pl.program_id(0) == 0)
    def _():
        right_ref[...] = both(right0_ref, right1_ref)

    block = transposed_times(both(left0_ref, left1_ref), right_ref[...])
    split_parity(block.astype(BF16), height, core, send_ref, keep_ref, 0)


def big_grad(core, left, right, size, block=256):
    rows, width = left[0].shape
    columns = right[0].shape[1]
    height = width // size
    groups = block // (2 * height)
    shape = jax.ShapeDtypeStruct((size // 2, height, columns), BF16)
    column = pl.BlockSpec((rows, block), lambda c: (0, c))
    whole = pl.BlockSpec((rows, columns), lambda c: (0, 0))
    spec = pl.BlockSpec((groups, height, columns), lambda c: (c, 0, 0))
    return pl.pallas_call(
        functools.partial(big_grad_kernel, height),
        grid=(width // block,),
        out_shape=(shape, shape),
        in_specs=[smem(), column, column, whole, whole],
        out_specs=(spec, spec),
        scratch_shapes=[pltpu.VMEM((2 * rows, columns), BF16)],
        compiler_params=pltpu.CompilerParams(vmem_limit_bytes=VMEM_LIMIT),
        cost_estimate=pl.CostEstimate(
            flops=4 * rows * width * columns, bytes_accessed=2 * width * columns, transcendentals=0
        ),
        name="big_grad",
    )(core, left[0], left[1], right[0], right[1])


def attend_back_kernel(
    own_ref,
    other_ref,
    attn_own_ref,
    attn_other_ref,
    resid_ref,
    grad_ref,
    query_ref,
    keys_ref,
    values_ref,
    lse_ref,
    w_query_ref,
    w_key_ref,
    w_value_ref,
    w_out_ref,
    vectors_ref,
    d_resid_ref,
    d_attn_ref,
    dq_ref,
    dk_ref,
    dv_ref,
    sums_ref,
    bias_sums_ref,
    part_ref,
    mix_ref,
    turned_ref,
    dq_turned_ref,
):
    d_act = own_ref[...].astype(F32) + other_ref[...].astype(F32)
    normed, inverse = layer_norm(resid_ref[...])
    d_resid = grad_ref[...] + norm_back(d_act * vectors_ref[4:5, :], normed, inverse)
    d_resid_ref[...] = d_resid
    d_attn = d_resid * vectors_ref[3:4, :]
    attn = attn_own_ref[...].astype(F32) + attn_other_ref[...].astype(F32) + vectors_ref[2:3, :]
    sums_ref[0:1, :] = row_sum(d_attn)
    sums_ref[1:2, :] = row_sum(d_resid * attn)
    sums_ref[2:3, :] = row_sum(d_act * normed)
    sums_ref[3:4, :] = row_sum(d_act)
    d_attn = d_attn.astype(BF16)
    d_attn_ref[...] = d_attn
    mix_ref[...] = times_transposed(d_attn, w_out_ref[...].astype(BF16)).astype(BF16)
    turned_ref[...] = keys_ref[...].astype(F32).T.astype(BF16)
    masks = half_masks()
    lane = lax.broadcasted_iota(jnp.int32, (1, LANES), 1)
    scale = 1.0 / math.sqrt(HEAD_DIM)

    def pair(index, carry):
        low = pl.multiple_of(index * LANES, LANES)
        query_pair = query_ref[:, pl.ds(low, LANES)]
        keys_pair = keys_ref[:, pl.ds(low, LANES)]
        values_pair = values_ref[:, pl.ds(low, LANES)]
        mix_pair = mix_ref[:, pl.ds(low, LANES)]
        found = []
        for half in range(2):
            scores = head_scores(keys_pair * masks[half], query_pair)
            probs = jnp.exp(scores - lse_ref[pl.ds(2 * index + half, 1), :])
            d_values = matmul(probs.astype(BF16), mix_pair)
            d_probs = times_transposed(values_pair * masks[half], mix_pair)
            delta = row_sum(probs * d_probs)
            d_scores = (probs * (d_probs - delta) * scale).astype(BF16)
            d_keys = matmul(d_scores, query_pair)
            at = pl.multiple_of(low + half * HEAD_DIM, HEAD_DIM)
            dq_turned_ref[pl.ds(at, HEAD_DIM), :] = matmul(
                turned_ref[pl.ds(at, HEAD_DIM), :], d_scores
            )
            found.append((d_values, d_keys))
        d_values = jnp.where(lane < HEAD_DIM, found[0][0], found[1][0])
        d_keys = jnp.where(lane < HEAD_DIM, found[0][1], found[1][1])
        bias_sums_ref[1:2, pl.ds(low, LANES)] = row_sum(d_values)
        dv_ref[:, pl.ds(low, LANES)] = d_values.astype(BF16)
        dk_ref[:, pl.ds(low, LANES)] = d_keys.astype(BF16)
        return carry

    lax.fori_loop(0, query_ref.shape[1] // LANES, pair, 0)
    d_query = dq_turned_ref[...].T
    bias_sums_ref[0:1, :] = row_sum(d_query)
    dq_ref[...] = d_query.astype(BF16)
    part = times_transposed(dq_ref[...], w_query_ref[...].astype(BF16))
    part += times_transposed(dk_ref[...], w_key_ref[...].astype(BF16))
    part += times_transposed(dv_ref[...], w_value_ref[...].astype(BF16))
    part_ref[...] = part.astype(BF16)


def attend_back(own, other, attn_own, attn_other, resid, grad, query, keys, values, lse, w_query, w_key, w_value, w_out, vectors):
    rows, width = resid.shape
    inner = query.shape[1]
    return pl.pallas_call(
        attend_back_kernel,
        out_shape=(
            jax.ShapeDtypeStruct((rows, width), F32),
            jax.ShapeDtypeStruct((rows, width), BF16),
            jax.ShapeDtypeStruct((rows, inner), BF16),
            jax.ShapeDtypeStruct((rows, inner), BF16),
            jax.ShapeDtypeStruct((rows, inner), BF16),
            jax.ShapeDtypeStruct((4, width), F32),
            jax.ShapeDtypeStruct((2, inner), F32),
            jax.ShapeDtypeStruct((rows, width), BF16),
        ),
        in_specs=[vmem()] * 15,
        out_specs=(vmem(),) * 8,
        scratch_shapes=[
            pltpu.VMEM((rows, inner), BF16),
            pltpu.VMEM((inner, rows), BF16),
            pltpu.VMEM((inner, rows), F32),
        ],
        compiler_params=pltpu.CompilerParams(vmem_limit_bytes=VMEM_LIMIT),
        cost_estimate=pl.CostEstimate(
            flops=20 * rows * width * inner, bytes_accessed=20 * width * inner, transcendentals=0
        ),
        name="attend_back",
    )(own, other, attn_own, attn_other, resid, grad, query, keys, values, lse, w_query, w_key, w_value, w_out, vectors)


def small_grad_kernel(
    heights,
    core_ref,
    act0,
    act1,
    dq0,
    dq1,
    dk0,
    dk1,
    dv0,
    dv1,
    mixed0,
    mixed1,
    da0,
    da1,
    send_a,
    keep_a,
    send_b,
    keep_b,
):
    core = core_ref[0]
    height, out_height = heights
    act = both(act0, act1)

    def put(block, rows, low, send_ref, keep_ref, first):
        for index in range(block.shape[0] // (2 * rows)):
            at = 2 * rows * index
            even, odd = block[at : at + rows], block[at + rows : at + 2 * rows]
            send_ref[first + index, low : low + rows, :] = jnp.where(core == 0, odd, even)
            keep_ref[first + index, low : low + rows, :] = jnp.where(core == 0, even, odd)

    pieces = ((dq0, dq1, 0, send_a, keep_a), (dk0, dk1, height, send_a, keep_a), (dv0, dv1, 0, send_b, keep_b))
    for first, second, low, send_ref, keep_ref in pieces:
        right = both(first, second)
        for start in range(0, act.shape[1], 256):
            block = transposed_times(act[:, start : start + 256], right).astype(BF16)
            put(block, height, low, send_ref, keep_ref, start // (2 * height))
    mixed, right = both(mixed0, mixed1), both(da0, da1)
    half = right.shape[1] // 2
    for start in range(0, mixed.shape[1], 256):
        block = transposed_times(mixed[:, start : start + 256], right).astype(BF16)
        first = start // (2 * out_height)
        put(block[:, :half], out_height, height, send_b, keep_b, first)
        put(block[:, half:], out_height, height + out_height, send_b, keep_b, first)


def small_grad(core, size, act, dq, dk, dv, mixed, da):
    inner, width = dq[0].shape[1], act[0].shape[1]
    height, out_height = width // size, inner // size
    shape = jax.ShapeDtypeStruct((size // 2, 2 * height, inner), BF16)
    rows = act[0].shape[0]
    return pl.pallas_call(
        functools.partial(small_grad_kernel, (height, out_height)),
        out_shape=(shape,) * 4,
        in_specs=[smem()] + [vmem()] * 12,
        out_specs=(vmem(),) * 4,
        compiler_params=pltpu.CompilerParams(vmem_limit_bytes=VMEM_LIMIT),
        cost_estimate=pl.CostEstimate(
            flops=16 * rows * width * inner, bytes_accessed=8 * width * inner, transcendentals=0
        ),
        name="small_grad",
    )(core, *act, *dq, *dk, *dv, *mixed, *da)


def finish_kernel(
    place_ref,
    resid0,
    resid1,
    mlp_own,
    mlp_other,
    d_resid0,
    d_resid1,
    d_act_own,
    d_act_other,
    rows0,
    rows1,
    grad0,
    grad1,
    vectors_ref,
    out_ref,
    d_out_ref,
    sums_ref,
    pad_ref,
):
    size = padded_rows()
    index = lax.broadcasted_iota(jnp.int32, (size, 1), 0)
    total = out_ref.shape[0]

    def put(block, slot):
        start = place_ref[2 * slot]
        live = place_ref[2 * slot + 1] > 0
        base = (start >> 3) << 3
        block = jnp.where((index < IMG_LEN) & live, block, 0.0)
        block = jnp.concatenate([block, jnp.zeros((SUBLANES, block.shape[1]), F32)], axis=0)
        block = pltpu.roll(block, start - base, axis=0)
        window = pl.ds(pl.multiple_of(base, SUBLANES), size + SUBLANES)
        pad_ref[window, :] += block

    pad_ref[...] = jnp.zeros(pad_ref.shape, F32)
    sums = [0.0, 0.0, 0.0, 0.0]
    for slot, (resid, grad) in enumerate(((resid0, grad0), (resid1, grad1))):
        part = slice(slot * size, (slot + 1) * size)
        mlp = mlp_own[part, :].astype(F32) + mlp_other[part, :].astype(F32) + vectors_ref[6:7, :]
        put(resid[...] + vectors_ref[7:8, :] * mlp, slot)
        sums[2] += row_sum(grad[...] * vectors_ref[7:8, :])
        sums[3] += row_sum(grad[...] * mlp)
    out_ref[...] = pad_ref[0:total, :]
    pad_ref[...] = jnp.zeros(pad_ref.shape, F32)
    for slot, (rows, d_resid) in enumerate(((rows0, d_resid0), (rows1, d_resid1))):
        part = slice(slot * size, (slot + 1) * size)
        d_act = d_act_own[part, :].astype(F32) + d_act_other[part, :].astype(F32)
        normed, inverse = layer_norm(rows[...])
        put(d_resid[...] + norm_back(d_act * vectors_ref[0:1, :], normed, inverse), slot)
        sums[0] += row_sum(d_act * normed)
        sums[1] += row_sum(d_act)
    d_out_ref[...] = pad_ref[0:total, :]
    for index_sum in range(4):
        sums_ref[index_sum : index_sum + 1, :] = sums[index_sum]


def finish(place, total, resid, mlp_own, mlp_other, d_resid, d_act_own, d_act_other, rows, grad, vectors):
    width = vectors.shape[1]
    return pl.pallas_call(
        finish_kernel,
        out_shape=(
            jax.ShapeDtypeStruct((total, width), F32),
            jax.ShapeDtypeStruct((total, width), F32),
            jax.ShapeDtypeStruct((4, width), F32),
        ),
        in_specs=[smem()] + [vmem()] * 13,
        out_specs=(vmem(),) * 3,
        scratch_shapes=[pltpu.VMEM((window_rows(total), width), F32)],
        compiler_params=pltpu.CompilerParams(vmem_limit_bytes=VMEM_LIMIT),
        cost_estimate=pl.CostEstimate(
            flops=40 * total * width, bytes_accessed=40 * total * width, transcendentals=0
        ),
        name="finish",
    )(place, *resid, mlp_own, mlp_other, *d_resid, d_act_own, d_act_other, *rows, *grad, vectors)


def newton_schulz(tall, x_ref, gram_ref, poly_ref, block=256, strip=512):
    side = gram_ref.shape[0]
    length = x_ref.shape[0] if tall else x_ref.shape[1]
    block, strip = min(block, side), min(strip, length)

    def gram_rows(low):
        if tall:
            return transposed_times(x_ref[:, low : low + block], x_ref[:, low:])
        return times_transposed(x_ref[low : low + block, :], x_ref[low:, :])

    def mirror(ref, low, rows):
        ref[low : low + block, low:] = rows
        for right in range(low + block, side, block):
            ref[right : right + block, low : low + block] = rows[
                :, right - low : right - low + block
            ].T

    def step(index, carry):
        for low in range(0, side, block):
            mirror(gram_ref, low, gram_rows(low).astype(jnp.bfloat16))
        for low in range(0, side, block):
            squares = matmul(gram_ref[low : low + block, :], gram_ref[:, low:])
            linear = gram_ref[low : low + block, low:].astype(jnp.float32)
            mirror(
                poly_ref, low, (poly_second * linear + poly_third * squares).astype(jnp.bfloat16)
            )
        for low in range(0, length, strip):
            part = (
                (slice(low, low + strip), slice(None))
                if tall
                else (slice(None), slice(low, low + strip))
            )
            old = x_ref[part]
            new = matmul(old, poly_ref[...]) if tall else matmul(poly_ref[...], old)
            x_ref[part] = (poly_first * old.astype(jnp.float32) + new).astype(jnp.bfloat16)
        return carry

    lax.fori_loop(0, 5, step, 0)


def ortho_kernel(tall, spots, in_ref, out_ref, x_ref, gram_ref, poly_ref):
    total = jnp.zeros((1, 1), jnp.float32)
    for (row, column, height, width), place, low in spots:
        piece = in_ref[place, low : low + height, :].astype(jnp.float32)
        total = total + jnp.sum(jnp.sum(piece * piece, axis=1, keepdims=True), axis=0, keepdims=True)
    norm = jnp.sqrt(total) + 1e-07
    for (row, column, height, width), place, low in spots:
        piece = in_ref[place, low : low + height, :].astype(jnp.float32)
        x_ref[row : row + height, column : column + width] = (piece / norm).astype(jnp.bfloat16)
    newton_schulz(tall, x_ref, gram_ref, poly_ref)
    for (row, column, height, width), place, low in spots:
        out_ref[place, low : low + height, :] = x_ref[
            row : row + height, column : column + width
        ]


def ortho_call(stack, shape, spots):
    tall = shape[0] > shape[1]
    side = min(shape)
    return pl.pallas_call(
        functools.partial(ortho_kernel, tall, spots),
        out_shape=jax.ShapeDtypeStruct(stack.shape, jnp.bfloat16),
        in_specs=[pl.BlockSpec(memory_space=pltpu.VMEM)],
        out_specs=pl.BlockSpec(memory_space=pltpu.VMEM),
        scratch_shapes=[
            pltpu.VMEM(shape, jnp.bfloat16),
            pltpu.VMEM((side, side), jnp.bfloat16),
            pltpu.VMEM((side, side), jnp.bfloat16),
        ],
        compiler_params=pltpu.CompilerParams(vmem_limit_bytes=48 * 1024 * 1024),
    )(stack)


class Grid:
    def __init__(self):
        self.size = lax.axis_size("dp")
        self.bits = self.size.bit_length() - 1
        self.me = lax.axis_index("dp")

    def bit(self, which):
        return (self.me >> which) & 1

    def swap(self, block, which):
        return lax.ppermute(
            block, "dp", [(d, d ^ (1 << which)) for d in range(self.size)]
        )

    def send(self, block, pairs):
        return lax.ppermute(block, "dp", pairs)


def pick(stack, index, axis):
    return lax.dynamic_index_in_dim(stack, index, axis, keepdims=False)


def scatter_sum(grid, sent, kept, order, done=()):
    rest = [b for b in range(grid.bits - 1, -1, -1) if b not in done]
    came = grid.swap(sent, done[-1])
    low = kept.dtype
    shape = (2,) * len(rest) + kept.shape[1:]
    kept, came = kept.reshape(shape), came.reshape(shape)
    for which in order:
        axis = rest.index(which)
        rest.pop(axis)
        mine = grid.bit(which)

        def side(index):
            total = pick(kept, index, axis).astype(F32) + pick(came, index, axis).astype(F32)
            return total.astype(low)

        sent = side(1 - mine)
        arrived = grid.swap(sent, which)
        kept, came = side(mine), arrived
    return kept.astype(F32) + came.astype(F32)


def to_root(grid, held, roots):
    others = [held]
    low = grid.size >> grid.high
    for step in range(1, 1 << grid.high):
        pairs = [(((r ^ step) * low) + c, r * low + c) for c, r in enumerate(roots)]
        others.append(grid.send(held, pairs))
    return jnp.stack(others)


def from_root(grid, stack, roots):
    low = grid.size >> grid.high
    root = jnp.array(roots, jnp.int32)[grid.me % low]
    step_here = (grid.me // low) ^ root
    mine = stack[0]
    for step in range(1, 1 << grid.high):
        pairs = [(r * low + c, ((r ^ step) * low) + c) for c, r in enumerate(roots)]
        came = grid.send(stack[step], pairs)
        mine = jnp.where(step_here == step, came, mine)
    return mine


def fold(block):
    half = block.shape[1] // 2
    return jnp.concatenate([block[:, :half], block[:, half:]], axis=0)


def unfold(block):
    half = block.shape[0] // 2
    return jnp.concatenate([block[:half], block[half:]], axis=1)


def pair_swap(block):
    count = lax.axis_size("tensor")
    return lax.ppermute(block, "tensor", [(t, t ^ 1) for t in range(count)])


def local(
    tokens,
    upstream,
    counts,
    offsets,
    w_query,
    w_key,
    w_value,
    w_out,
    w_up,
    w_down,
    vectors,
    attn_bias,
    up_bias,
    mom_query,
    mom_key,
    mom_value,
    mom_out,
    mom_up,
    mom_down,
    mom_vectors,
    mom_attn_bias,
    mom_up_bias,
):
    params = (w_query, w_key, w_value, w_out, w_up, w_down, vectors, attn_bias, up_bias)
    image_count = counts[0]
    starts = [offsets[0, slot] for slot in range(SLOTS)]
    lives = [(slot < image_count).astype(jnp.int32) for slot in range(SLOTS)]
    places = [jnp.stack([s, v]) for s, v in zip(starts, lives)]

    grid = Grid()
    size, bits, me = grid.size, grid.bits, grid.me
    core_here = grid.bit(0).reshape(1)
    bf16 = jnp.bfloat16

    forward, attn_parts, feeds = [], [], []
    for slot in range(SLOTS):
        found = attend(places[slot], tokens, w_query, w_key, w_value, w_out, vectors, attn_bias)
        forward.append(found)
        attn_parts.append((found[7], pair_swap(found[7])))
    for slot in range(SLOTS):
        feeds.append(
            feed(
                places[slot],
                *attn_parts[slot],
                forward[slot][0],
                upstream,
                vectors,
                up_bias.reshape(1, -1),
                w_up,
                w_down,
            )
        )
    image_rows = [f[0] for f in forward]
    acts, queries, keys, values, mixed, lses = ([f[i] for f in forward] for i in range(1, 7))
    resids, grad_rows, acts2, d_mlps, activs, d_pres, upb_sums, d_act2s, mlps = (
        [f[i] for f in feeds] for i in range(9)
    )
    d_act2_pairs = [(d, pair_swap(d)) for d in d_act2s]
    up_terms = big_grad(core_here, acts2, d_pres, size)
    down_terms = big_grad(core_here, activs, d_mlps, size)
    order_a = list(range(1, bits))
    order_b = list(range(2, bits)) + [1]
    g_up = scatter_sum(grid, *up_terms, order_a, (0,))
    g_down = scatter_sum(grid, *down_terms, order_b, (0,))
    mlp_own = jnp.concatenate(mlps, axis=0)
    mlp_other = pair_swap(mlp_own)

    backs = []
    for slot in range(SLOTS):
        backs.append(
            attend_back(
                *d_act2_pairs[slot],
                *attn_parts[slot],
                resids[slot],
                grad_rows[slot],
                queries[slot],
                keys[slot],
                values[slot],
                lses[slot],
                w_query,
                w_key,
                w_value,
                w_out,
                vectors,
            )
        )
    d_resids, d_attns, dqs, dks, dvs, back_sums, bias_sums, d_act1s = (
        [f[i] for f in backs] for i in range(8)
    )
    send_a, keep_a, send_b, keep_b = small_grad(
        core_here, size, acts, dqs, dks, dvs, mixed, d_attns
    )
    g_first = scatter_sum(grid, send_a, keep_a, order_a, (0,))
    g_second = scatter_sum(grid, send_b, keep_b, order_b, (0,))
    height = w_query.shape[0] // size
    g_query, g_key = g_first[:height], g_first[height:]
    g_value, g_out = g_second[:height], unfold(g_second[height:])
    d_act1_own = jnp.concatenate(d_act1s, axis=0)
    d_act1_other = pair_swap(d_act1_own)
    block_out, grad_tokens, end_sums = finish(
        jnp.concatenate(places),
        tokens.shape[0],
        resids,
        mlp_own,
        mlp_other,
        d_resids,
        d_act1_own,
        d_act1_other,
        image_rows,
        grad_rows,
        vectors,
    )
    middle = back_sums[0] + back_sums[1]
    vec_sums = jnp.concatenate([end_sums[:2], middle, end_sums[2:]], axis=0)
    bias_sum = bias_sums[0] + bias_sums[1]
    upb_sum = upb_sums[0] + upb_sums[1]

    def own_rows(full):
        width = full.shape[0] // size
        return lax.dynamic_slice_in_dim(full, me * width, width, 0)

    def own_columns(full):
        return own_rows(full.T).T

    def by_columns(full):
        count, width = full.shape
        return full.reshape(count, size, width // size).transpose(1, 0, 2).reshape(size, -1)

    vec_part, bias_part, upb_part = by_columns(vec_sums), by_columns(bias_sum), by_columns(upb_sum)
    packed = jnp.concatenate([vec_part, bias_part, upb_part], axis=1)
    fill = -packed.shape[1] % LANES
    packed = jnp.pad(packed, ((0, 0), (0, fill))).reshape(size // 2, 2, -1, LANES)
    small = scatter_sum(
        grid,
        pick(packed, 1 - grid.bit(0), 1),
        pick(packed, grid.bit(0), 1),
        order_a,
        (0,),
    ).reshape(-1)
    n_vec, n_bias, n_upb = vec_part.shape[1], bias_part.shape[1], upb_part.shape[1]
    grad_vec = small[:n_vec].reshape(vectors.shape[0], -1)
    grad_bias = small[n_vec : n_vec + n_bias].reshape(attn_bias.shape[0], -1)
    grad_upb = small[n_vec + n_bias : n_vec + n_bias + n_upb]

    grad_shares = (g_query, g_key, g_value, g_out, g_up, g_down)
    old_moments = (mom_query, mom_key, mom_value, mom_out, mom_up, mom_down)
    next_mats = tuple((momentum_beta * m + g for m, g in zip(old_moments, grad_shares)))
    next_vec = momentum_beta * mom_vectors + grad_vec
    next_bias = momentum_beta * mom_attn_bias + grad_bias
    next_upb = momentum_beta * mom_up_bias + grad_upb
    low = tuple((m.astype(bf16) for m in next_mats))

    grid.high = bits - 2
    highs = 1 << grid.high
    column, core = grid.bit(1), grid.bit(0)
    high_a, high_b = min(1, highs - 1), min(2, highs - 1)

    big_roots = (high_a, high_a, high_b, high_b)
    up_share, down_share = fold(low[4]), low[5]
    keep = jnp.where(column == 0, up_share, down_share)
    came = grid.swap(jnp.where(column == 0, down_share, up_share), 1)
    held = to_root(grid, jnp.stack([keep, came]), big_roots)
    big_stack = jnp.stack([held, grid.send(held, [((r << 2) | (c << 1) | 1, (r << 2) | (c << 1)) for c, r in ((0, high_a), (1, high_b))])])
    up_root, down_root = high_a << 2, (high_b << 2) | 2

    small_roots = (high_b, high_a, high_a, high_b)
    shares = [low[0], low[1], low[2], fold(low[3])]
    first_pair, second_pair = jnp.stack(shares[:2]), jnp.stack(shares[2:])
    keep = jnp.where(column == 0, first_pair, second_pair)
    came = grid.swap(jnp.where(column == 0, second_pair, first_pair), 1)
    two = jnp.stack([keep, came], axis=1)
    keep = pick(two, core, 0)
    came = grid.swap(pick(two, 1 - core, 0), 0)
    small_stack = to_root(grid, jnp.stack([keep, came]), small_roots)
    small_devices = [(r << 2) | c for c, r in enumerate(small_roots)]

    def big_spots(root, shape, folded):
        height, width = shape[0] // size, shape[1]
        spots = []
        for d in range(size):
            place = (
                ((d & 1) ^ (root & 1)) * highs + ((d >> 2) ^ (root >> 2))
            ) * 2 + (((d >> 1) ^ (root >> 1)) & 1)
            if folded:
                spots.append(((d * height, 0, height, width // 2), place, 0))
                spots.append(((d * height, width // 2, height, width // 2), place, height))
            else:
                spots.append(((d * height, 0, height, width), place, 0))
        return spots

    def small_spots(root, shape, folded):
        height, width = shape[0] // size, shape[1]
        spots = []
        for d in range(size):
            place = (
                ((d >> 2) ^ (root >> 2)) * 2 + ((d & 1) ^ (root & 1))
            ) * 2 + (((d >> 1) ^ (root >> 1)) & 1)
            if folded:
                spots.append(((d * height, 0, height, width // 2), place, 0))
                spots.append(((d * height, width // 2, height, width // 2), place, height))
            else:
                spots.append(((d * height, 0, height, width), place, 0))
        return spots

    def flat(stack):
        return stack.reshape((-1,) + stack.shape[-2:])

    role = jnp.where(me == up_root, 1, jnp.where(me == down_root, 2, 0))
    big_flat = lax.switch(
        role,
        [
            lambda s: s,
            lambda s: ortho_call(s, w_up.shape, big_spots(up_root, w_up.shape, True)),
            lambda s: ortho_call(s, w_down.shape, big_spots(down_root, w_down.shape, False)),
        ],
        flat(big_stack),
    )
    role = jnp.where(
        me == small_devices[3],
        4,
        jnp.where(
            me == small_devices[0],
            1,
            jnp.where(me == small_devices[1], 2, jnp.where(me == small_devices[2], 3, 0)),
        ),
    )
    small_flat = lax.switch(
        role,
        [lambda s: s]
        + [
            functools.partial(
                lambda root, s: ortho_call(s, w_query.shape, small_spots(root, w_query.shape, False)),
                root,
            )
            for root in small_devices[:3]
        ]
        + [
            lambda s: ortho_call(
                s, w_out.shape, small_spots(small_devices[3], w_out.shape, True)
            )
        ],
        flat(small_stack),
    )

    big = big_flat.reshape(big_stack.shape)
    came = grid.send(big[1], [((r << 2) | (c << 1), (r << 2) | (c << 1) | 1) for c, r in ((0, high_a), (1, high_b))])
    held = jnp.where(core == 0, big[0], came)
    held = from_root(grid, held, big_roots)
    came = grid.swap(held[1], 1)
    up_ortho = unfold(jnp.where(column == 0, held[0], came))
    down_ortho = jnp.where(column == 0, came, held[0])

    held = from_root(grid, small_flat.reshape(small_stack.shape), small_roots)
    came = grid.swap(held[1], 0)
    two = jnp.where(core == 0, jnp.stack([held[0], came]), jnp.stack([came, held[0]]))
    came = grid.swap(two[:, 1], 1)
    first_pair = jnp.where(column == 0, two[:, 0], came)
    second_pair = jnp.where(column == 0, came, two[:, 0])
    orthos = (
        first_pair[0],
        first_pair[1],
        second_pair[0],
        unfold(second_pair[1]),
        up_ortho,
        down_ortho,
    )
    rates = (1.0, 1.0, 1.0, 1.0, math.sqrt(max(1.0, FF / D)), 1.0)
    updated = []
    for slot in range(6):
        updated.append(
            own_rows(params[slot]) - matrix_rate * rates[slot] * orthos[slot].astype(jnp.float32)
        )
    new_vectors = own_columns(vectors) - vector_rate * next_vec
    new_bias = own_columns(attn_bias) - vector_rate * next_bias
    new_upb = own_rows(up_bias) - vector_rate * next_upb
    return (
        block_out,
        grad_tokens,
        *grad_shares,
        grad_vec,
        grad_bias,
        grad_upb,
        *updated,
        new_vectors,
        new_bias,
        new_upb,
        *next_mats,
        next_vec,
        next_bias,
        next_upb,
    )


def solution(mesh):
    placed = (
        P("dp", None),
        P("dp", None),
        P("dp"),
        P("dp", None),
        P(None, "tensor"),
        P(None, "tensor"),
        P(None, "tensor"),
        P("tensor", None),
        P(None, "tensor"),
        P("tensor", None),
        P(),
        P(None, "tensor"),
        P("tensor"),
        P("dp", "tensor"),
        P("dp", "tensor"),
        P("dp", "tensor"),
        P(("tensor", "dp"), None),
        P("dp", "tensor"),
        P(("tensor", "dp"), None),
        P(None, "dp"),
        P(None, ("tensor", "dp")),
        P(("tensor", "dp")),
    )
    return jax.shard_map(
        local,
        mesh=mesh,
        in_specs=placed,
        out_specs=(
            P("dp", None),
            P("dp", None),
            P("dp", "tensor"),
            P("dp", "tensor"),
            P("dp", "tensor"),
            P(("tensor", "dp"), None),
            P("dp", "tensor"),
            P(("tensor", "dp"), None),
            P(None, "dp"),
            P(None, ("tensor", "dp")),
            P(("tensor", "dp")),
            P("dp", "tensor"),
            P("dp", "tensor"),
            P("dp", "tensor"),
            P(("tensor", "dp"), None),
            P("dp", "tensor"),
            P(("tensor", "dp"), None),
            P(None, "dp"),
            P(None, ("tensor", "dp")),
            P(("tensor", "dp")),
            P("dp", "tensor"),
            P("dp", "tensor"),
            P("dp", "tensor"),
            P(("tensor", "dp"), None),
            P("dp", "tensor"),
            P(("tensor", "dp"), None),
            P(None, "dp"),
            P(None, ("tensor", "dp")),
            P(("tensor", "dp")),
        ),
        check_vma=False,
    )
```
